256 devices in a mesh: row: 16 (over x, y), col: 16 (over z, core).
Axes of the slice: x: 4, y: 4, z: 8, core: 2. Of those that a mesh axis runs over, the one named last changes fastest.
Arguments:
- queries: bfloat16 [32768, 2048], P(('row', 'col')), may hold values from -6 to 6
- keys: bfloat16 [32768, 2048], P(('row', 'col')), may hold values from -6 to 6
- values: bfloat16 [32768, 2048], P(('row', 'col')), may hold values from -6 to 6
- grad_out: bfloat16 [32768, 2048], P(('row', 'col')), may hold values from -6 to 6
- conv_weight: float32 [4, 2048], replicated, may hold values from -3 to 3
Outputs:
- grad_queries: bfloat16 [32768, 2048], P(('row', 'col'))
- grad_keys: bfloat16 [32768, 2048], P(('row', 'col'))
- grad_values: bfloat16 [32768, 2048], P(('row', 'col'))
- grad_weight: float32 [4, 2048], replicated
The draws below stay inside these ranges and needn't reach their ends.
All inputs are finite; a program needn't handle non-finite values.
Results may differ from the reference program's by a relative error of at most 0.025.
Values may be sent and summed in bfloat16 or wider, within the bound.
A program may use at most 192 MiB of HBM per device.

```python
import jax
import jax.numpy as jnp
from jax import lax

HEADS = 16
DH = 128
CW = 4
TOK_DEV = 128
D = 2048
TOKENS = 32768


def steps_of(own_key, shape, cuts, smallest, high):
    level, own = 1.0, jax.random.fold_in(own_key, 6)
    for dim, blocks in cuts:
        heights = jnp.exp(jax.random.uniform(jax.random.fold_in(own, dim), (blocks,), jnp.float32, smallest / len(cuts), high / len(cuts)))
        level = level * jnp.repeat(heights, shape[dim] // blocks).reshape([-1 if axis == dim else 1 for axis in range(len(shape))])
    return level


def gaussian(key, dims, width, limit, pieces=(), dtype=jnp.bfloat16):
    entries = width * jax.random.normal(key, dims, jnp.float32)
    if pieces:
        entries = entries * steps_of(key, dims, pieces, -0.22, 0.18)
    return jnp.clip(entries, -limit, limit).astype(dtype)


def setup_inputs(seed: int = 0) -> dict:
    arg_keys = jax.random.split(jax.random.key(seed), 6)
    return {
        "queries": gaussian(arg_keys[0], (TOKENS, D), 1.0, 6.0, ((0, 256),)),
        "keys": gaussian(arg_keys[1], (TOKENS, D), 1.0, 6.0, ((0, 256),)),
        "values": gaussian(arg_keys[2], (TOKENS, D), 1.0, 6.0, ((0, 256),)),
        "grad_out": gaussian(arg_keys[3], (TOKENS, D), 1.0, 6.0, ((0, 256),)),
        "conv_weight": gaussian(arg_keys[4], (CW, D), 0.5, 3.0, (), jnp.float32),
    }


def reference(queries, keys, values, grad_out, conv_weight):
    total = queries.shape[0]
    rows = TOK_DEV
    blocks = total // rows
    scale = (DH * total) ** -0.5
    value_pad = jnp.pad(values.astype(jnp.float32), ((CW - 1, 0), (0, 0)))
    conv_acc = jnp.zeros((total, HEADS * DH), jnp.float32)
    for offset in range(CW):
        conv_acc = conv_acc + conv_weight[offset][None, :] * value_pad[CW - 1 - offset:CW - 1 - offset + total]
    conved = conv_acc.astype(jnp.bfloat16)
    query_blocks = queries.reshape(blocks, rows, HEADS, DH)
    key_blocks = keys.reshape(blocks, rows, HEADS, DH)
    conv_blocks = conved.reshape(blocks, rows, HEADS, DH)
    grad_blocks = grad_out.reshape(blocks, rows, HEADS, DH)

    def local_states(items):
        query_part, key_part, conv_part, grad_part = items
        key_state = jnp.einsum("thd,the->hde", key_part.astype(jnp.float32), conv_part.astype(jnp.float32))
        query_state = jnp.einsum("thd,the->hde", query_part.astype(jnp.float32), grad_part.astype(jnp.float32))
        return key_state, query_state

    key_states, query_states = lax.map(local_states, (query_blocks, key_blocks, conv_blocks, grad_blocks))
    zero_state = jnp.zeros((HEADS, DH, DH), jnp.float32)

    def carry_on(carry, state):
        return carry + state, carry

    _, prefix = lax.scan(carry_on, zero_state, key_states)
    _, suffix = lax.scan(carry_on, zero_state, query_states, reverse=True)
    positions = jnp.arange(rows)
    causal = (positions[:, None] >= positions[None, :])[None, :, :]

    def block_grads(items):
        query_part, key_part, conv_part, grad_part, prefix_part, suffix_part = items
        query_f = query_part.astype(jnp.float32)
        key_f = key_part.astype(jnp.float32)
        conv_f = conv_part.astype(jnp.float32)
        grad_f = grad_part.astype(jnp.float32)
        attn = jnp.where(causal, jnp.einsum("thd,uhd->htu", grad_f, conv_f), 0.0).astype(jnp.bfloat16).astype(jnp.float32)
        score = jnp.where(causal, jnp.einsum("thd,uhd->htu", query_f, key_f), 0.0).astype(jnp.bfloat16).astype(jnp.float32)
        prefix_f = prefix_part.astype(jnp.bfloat16).astype(jnp.float32)
        suffix_f = suffix_part.astype(jnp.bfloat16).astype(jnp.float32)
        grad_query = scale * (jnp.einsum("htu,uhd->thd", attn, key_f) + jnp.einsum("the,hde->thd", grad_f, prefix_f))
        grad_key = scale * (jnp.einsum("htu,thd->uhd", attn, query_f) + jnp.einsum("the,hde->thd", conv_f, suffix_f))
        grad_conv = scale * (jnp.einsum("htu,thd->uhd", score, grad_f) + jnp.einsum("thd,hde->the", key_f, suffix_f))
        return grad_query.astype(jnp.bfloat16), grad_key.astype(jnp.bfloat16), grad_conv

    grad_query, grad_key, grad_conv = lax.map(block_grads, (query_blocks, key_blocks, conv_blocks, grad_blocks, prefix, suffix))
    grad_query = grad_query.reshape(total, HEADS * DH)
    grad_key = grad_key.reshape(total, HEADS * DH)
    grad_conv = grad_conv.reshape(total, HEADS * DH)
    grad_pad = jnp.pad(grad_conv, ((0, CW - 1), (0, 0)))
    value_acc = jnp.zeros((total, HEADS * DH), jnp.float32)
    weight_rows = []
    for offset in range(CW):
        value_acc = value_acc + conv_weight[offset][None, :] * grad_pad[offset:offset + total]
        weight_rows.append(jnp.sum(grad_conv * value_pad[CW - 1 - offset:CW - 1 - offset + total], axis=0))
    grad_weight = jnp.stack(weight_rows, axis=0)
    return grad_query, grad_key, value_acc.astype(jnp.bfloat16), grad_weight
```

```python
import functools

import jax
import jax.numpy as jnp
from jax import lax
from jax.experimental import pallas as pl
from jax.experimental.pallas import tpu as pltpu
from jax.sharding import PartitionSpec as P

DH = 128
CW = 4
PAD = 8
TAIL = 16
MESH = pl.DeviceIdType.MESH
F32 = jnp.float32
BF16 = jnp.bfloat16
KEY, QUERY = 0, 1


def dot(a, b, contract):
    return lax.dot_general(a, b, ((contract[:1], contract[1:]), ((), ())), preferred_element_type=F32)


def kernel(
    nr, nc, scale,
    q_in, k_in, v_in, g_in, w_ref,
    gq_out, gk_out, gv_out, gw_out,
    q, k, v, g, conv, vext, vhalo, gext, ghalo, gq_part, gk_part, gq_v, gk_v, gv_v,
    state, sib_state, pair, zstate, total, rstate, back, zback, fwd, final,
    gw_part, gw_col, gw_row_src, gw_row, gw_all_src, gw_all, gw_v,
    sib_s, sib_r, zf_s, zf_r, row_s, row_r, zb_s, zb_r, sb_s, sb_r, halo_s, halo_r,
    cw_s, cw_r, rw_s, rw_r, aw_s, aw_r, in_sem, out_sem,
):
    r, c = lax.axis_index("row"), lax.axis_index("col")
    nz = nc // 2
    z, j = c // 2, c % 2
    rows, width = q.shape
    heads = width // DH
    sib = (r, 2 * z + (1 - j))
    place = r * nc + c
    blocks = nr * nc
    after, before = (place + 1) % blocks, (place + blocks - 1) % blocks
    after, before = (after // nc, after % nc), (before // nc, before % nc)
    far_first = sorted(range(1, nz), key=lambda o: -min(o, nz - o))
    near_first = far_first[::-1]

    def send(src, dst, ss, rs, to):
        return pltpu.make_async_remote_copy(src_ref=src, dst_ref=dst, send_sem=ss, recv_sem=rs, device_id=to, device_id_type=MESH)

    def at(o):
        return (z + o) % nz

    def lanes(h):
        return pl.ds(pl.multiple_of(h * DH, DH), DH)

    def each_head(fn, together=4):
        def some(i, carry):
            for u in range(together):
                fn(i * together + u)
            return carry

        lax.fori_loop(0, heads // together, some, 0)

    barrier = pltpu.get_barrier_semaphore()

    def greet(to):
        pl.semaphore_signal(barrier, inc=1, device_id=to, device_id_type=MESH)

    loads = [
        pltpu.make_async_copy(src, dst, in_sem.at[i])
        for i, (src, dst) in enumerate(((q_in, q), (g_in, g), (v_in, v), (k_in, k)))
    ]
    for load in loads:
        load.start()
    lax.fori_loop(1, nc, lambda o, x: (greet((r, (c + o) % nc)), x)[1], 0)
    lax.fori_loop(1, nr, lambda o, x: (greet(((r + o) % nr, c)), x)[1], 0)
    greet(after)
    greet(before)

    loads[0].wait()
    loads[1].wait()

    def query_state(h):
        state[QUERY, h] = dot(q[:, lanes(h)], g[:, lanes(h)], (0, 0)).astype(BF16)

    each_head(query_state)
    loads[2].wait()
    loads[3].wait()
    pl.semaphore_wait(barrier, nc - 1 + nr - 1 + 2)

    vsend = send(v.at[pl.ds(rows - TAIL, TAIL)], vhalo, halo_s.at[0], halo_r.at[0], after)
    vsend.start()

    def to_sibling(kind, zz):
        send(
            state.at[kind, 2 * zz + (1 - j)], sib_state.at[kind, zz], sib_s.at[kind, zz], sib_r.at[kind, zz], sib
        ).start()

    for o in far_first + [0]:
        to_sibling(QUERY, at(o))

    above = lax.broadcasted_iota(jnp.int32, (rows, rows), 0) <= lax.broadcasted_iota(jnp.int32, (rows, rows), 1)
    below = lax.broadcasted_iota(jnp.int32, (rows, rows), 0) >= lax.broadcasted_iota(jnp.int32, (rows, rows), 1)

    def score_part(h):
        score = jnp.where(above, dot(k[:, lanes(h)], q[:, lanes(h)], (1, 1)), 0.0).astype(BF16)
        gext[pl.ds(0, rows), lanes(h)] = dot(score, g[:, lanes(h)], (1, 0))

    each_head(score_part)

    def pair_up(kind):
        for o in far_first + [0]:
            zz = at(o)
            send(state.at[kind, 0], sib_state.at[kind, zz], sib_s.at[kind, zz], sib_r.at[kind, zz], sib).wait_recv()
            both = state[kind, 2 * zz + j].astype(F32) + sib_state[kind, zz].astype(F32)
            if o == 0:
                zstate[kind, zz] = both.astype(BF16)
            else:
                pair[kind, zz] = both.astype(BF16)
                send(
                    pair.at[kind, zz], zstate.at[kind, z], zf_s.at[kind, zz], zf_r.at[kind, z], (r, 2 * zz + j)
                ).start()

    pair_up(QUERY)

    send(v.at[pl.ds(rows - TAIL, TAIL)], vhalo, halo_s.at[0], halo_r.at[0], after).wait_recv()
    vext[pl.ds(0, PAD)] = jnp.where(place > 0, vhalo[pl.ds(TAIL - PAD, PAD)].astype(F32), 0.0)
    vext[pl.ds(PAD, rows)] = v[...].astype(F32)

    def convolve(h):
        total_ = jnp.zeros((rows, DH), F32)
        for tap in range(CW):
            total_ = total_ + w_ref[pl.ds(tap, 1), lanes(h)] * vext[pl.ds(PAD - tap, rows), lanes(h)]
        conv[:, lanes(h)] = total_.astype(BF16)

    def key_state(h):
        convolve(h)
        state[KEY, h] = dot(k[:, lanes(h)], conv[:, lanes(h)], (0, 0)).astype(BF16)

    for o in far_first + [0]:
        zz = at(o)
        key_state(2 * zz + (1 - j))
        to_sibling(KEY, zz)
    lax.fori_loop(0, nz, lambda i, x: (key_state(2 * i + j), x)[1], 0)
    pair_up(KEY)

    def attn_part(h):
        attn = jnp.where(below, dot(g[:, lanes(h)], conv[:, lanes(h)], (1, 1)), 0.0).astype(BF16)
        gq_part[:, lanes(h)] = dot(attn, k[:, lanes(h)], (1, 0))
        attn_t = jnp.where(above, dot(conv[:, lanes(h)], g[:, lanes(h)], (1, 1)), 0.0).astype(BF16)
        gk_part[:, lanes(h)] = dot(attn_t, q[:, lanes(h)], (1, 0))

    each_head(attn_part)

    def run_total(kind):
        acc = zstate[kind, z].astype(F32)
        for o in near_first:
            zz = at(o)
            send(pair.at[kind, 0], zstate.at[kind, zz], zf_s.at[kind, zz], zf_r.at[kind, zz], sib).wait_recv()
            acc = acc + zstate[kind, zz].astype(F32)
        total[kind] = acc.astype(BF16)

        def one(rr, x):
            send(total.at[kind], rstate.at[r], row_s.at[rr], row_r.at[r], (rr, c)).start()
            return x

        if kind == KEY:
            lax.fori_loop(r + 1, nr, one, 0)
        else:
            lax.fori_loop(0, r, one, 0)

    run_total(QUERY)
    run_total(KEY)

    def spread(kind):
        def one(rr, acc):
            send(total.at[kind], rstate.at[rr], row_s.at[rr], row_r.at[rr], sib).wait_recv()
            return acc + rstate[rr].astype(F32)

        acc = jnp.zeros((DH, DH), F32)
        acc = lax.fori_loop(0, r, one, acc) if kind == KEY else lax.fori_loop(r + 1, nr, one, acc)
        for zz in range(nz) if kind == KEY else reversed(range(nz)):
            back[kind, zz] = acc.astype(BF16)
            acc = acc + zstate[kind, zz].astype(F32)
        for o in far_first:
            zz = at(o)
            send(
                back.at[kind, zz], zback.at[kind, z], zb_s.at[kind, zz], zb_r.at[kind, z], (r, 2 * zz + j)
            ).start()

    spread(QUERY)
    spread(KEY)

    mine_too = {KEY: j.astype(F32), QUERY: (1 - j).astype(F32)}

    def arrive(kind, o):
        zz = at(o)
        h = 2 * zz + j
        if o == 0:
            chip = back[kind, zz].astype(F32)
        else:
            send(back.at[kind, 0], zback.at[kind, zz], zb_s.at[kind, zz], zb_r.at[kind, zz], sib).wait_recv()
            chip = zback[kind, zz].astype(F32)
        fwd[kind, zz] = (chip + (1.0 - mine_too[kind]) * state[kind, h].astype(F32)).astype(BF16)
        send(fwd.at[kind, zz], final.at[kind, h], sb_s.at[kind, zz], sb_r.at[kind, zz], sib).start()
        final[kind, h] = (chip + mine_too[kind] * sib_state[kind, zz].astype(F32)).astype(BF16)
        return h

    def arrive_other(kind, o):
        zz = at(o)
        h = 2 * zz + (1 - j)
        send(fwd.at[kind, 0], final.at[kind, h], sb_s.at[kind, zz], sb_r.at[kind, zz], sib).wait_recv()
        return h

    gw_part[...] = jnp.zeros_like(gw_part)

    def with_suffix(h):
        suffix = final[QUERY, h]
        grad_conv = scale * (gext[pl.ds(0, rows), lanes(h)] + dot(k[:, lanes(h)], suffix, (1, 0)))
        gext[pl.ds(0, rows), lanes(h)] = grad_conv
        grad_key = scale * (gk_part[:, lanes(h)] + dot(conv[:, lanes(h)], suffix, (1, 1)))
        gk_v[:, lanes(h)] = grad_key.astype(BF16)
        for tap in range(CW):
            gw_part[h, pl.ds(tap, 1)] = jnp.sum(
                grad_conv * vext[pl.ds(PAD - tap, rows), lanes(h)], axis=0, keepdims=True
            )

    def weight_to_owner(h):
        send(gw_part.at[h], gw_col.at[c], cw_s.at[h], cw_r.at[c], (r, h)).start()

    for o in [0] + near_first:
        h = arrive(QUERY, o)
        with_suffix(h)
        if o == 0:
            gw_col[c] = gw_part[h]
        else:
            weight_to_owner(h)
    for o in [0] + near_first:
        h = arrive_other(QUERY, o)
        with_suffix(h)
        weight_to_owner(h)
    gsend = send(gext.at[pl.ds(0, PAD)], ghalo, halo_s.at[1], halo_r.at[1], before)
    gsend.start()
    gk_store = pltpu.make_async_copy(gk_v, gk_out, out_sem.at[0])
    gk_store.start()

    def from_col(o, acc):
        cc = (c + o) % nc
        send(gw_part.at[0], gw_col.at[cc], cw_s.at[cc], cw_r.at[cc], sib).wait_recv()
        return acc

    lax.fori_loop(1, nc, from_col, 0)
    gw_row_src[...] = jnp.sum(gw_col[...], axis=0)
    gw_row[r] = gw_row_src[...]

    def to_row(o, x):
        rr = (r + o) % nr
        send(gw_row_src, gw_row.at[r], rw_s.at[rr], rw_r.at[r], (rr, c)).start()
        return x

    lax.fori_loop(1, nr, to_row, 0)

    def with_prefix(h):
        grad_query = scale * (gq_part[:, lanes(h)] + dot(g[:, lanes(h)], final[KEY, h], (1, 1)))
        gq_v[:, lanes(h)] = grad_query.astype(BF16)

    for o in [0] + near_first:
        with_prefix(arrive(KEY, o))

    def from_row(o, x):
        rr = (r + o) % nr
        send(gw_row_src, gw_row.at[rr], rw_s.at[rr], rw_r.at[rr], sib).wait_recv()
        return x

    lax.fori_loop(1, nr, from_row, 0)
    gw_all_src[...] = jnp.sum(gw_row[...], axis=0)
    gw_all[c] = gw_all_src[...]

    def to_col(o, x):
        cc = (c + o) % nc
        send(gw_all_src, gw_all.at[c], aw_s.at[cc], aw_r.at[c], (r, cc)).start()
        return x

    lax.fori_loop(1, nc, to_col, 0)

    for o in [0] + near_first:
        with_prefix(arrive_other(KEY, o))
    gq_store = pltpu.make_async_copy(gq_v, gq_out, out_sem.at[1])
    gq_store.start()

    gsend.wait_recv()
    gext[pl.ds(rows, PAD)] = jnp.where(place < blocks - 1, ghalo[...], 0.0)

    def value_part(h):
        acc = jnp.zeros((rows, DH), F32)
        for tap in range(CW):
            acc = acc + w_ref[pl.ds(tap, 1), lanes(h)] * gext[pl.ds(tap, rows), lanes(h)]
        gv_v[:, lanes(h)] = acc.astype(BF16)

    each_head(value_part)
    gv_store = pltpu.make_async_copy(gv_v, gv_out, out_sem.at[2])
    gv_store.start()

    def from_all(o, x):
        cc = (c + o) % nc
        send(gw_all_src, gw_all.at[cc], aw_s.at[cc], aw_r.at[cc], sib).wait_recv()
        return x

    lax.fori_loop(1, nc, from_all, 0)
    for h in range(heads):
        gw_v[:, h * DH : (h + 1) * DH] = gw_all[h][:CW]
    gw_store = pltpu.make_async_copy(gw_v, gw_out, out_sem.at[3])
    gw_store.start()

    vsend.wait_send()
    gsend.wait_send()
    for kind in (KEY, QUERY):

        def sib_sent(i, x):
            send(state.at[kind, 0], sib_state.at[kind, 0], sib_s.at[kind, i], sib_r.at[kind, i], sib).wait_send()
            send(fwd.at[kind, 0], final.at[kind, 0], sb_s.at[kind, i], sb_r.at[kind, i], sib).wait_send()
            return x

        def z_sent(o, x):
            zz = (z + o) % nz
            send(pair.at[kind, 0], zstate.at[kind, 0], zf_s.at[kind, zz], zf_r.at[kind, zz], sib).wait_send()
            send(back.at[kind, 0], zback.at[kind, 0], zb_s.at[kind, zz], zb_r.at[kind, zz], sib).wait_send()
            return x

        lax.fori_loop(0, nz, sib_sent, 0)
        lax.fori_loop(1, nz, z_sent, 0)

    def row_sent(o, x):
        rr = (r + o) % nr
        send(total.at[0], rstate.at[0], row_s.at[rr], row_r.at[rr], sib).wait_send()
        send(gw_row_src, gw_row.at[0], rw_s.at[rr], rw_r.at[rr], sib).wait_send()
        return x

    def col_sent(o, x):
        cc = (c + o) % nc
        send(gw_part.at[0], gw_col.at[0], cw_s.at[cc], cw_r.at[cc], sib).wait_send()
        send(gw_all_src, gw_all.at[0], aw_s.at[cc], aw_r.at[cc], sib).wait_send()
        return x

    lax.fori_loop(1, nr, row_sent, 0)
    lax.fori_loop(1, nc, col_sent, 0)
    for store in (gk_store, gq_store, gv_store, gw_store):
        store.wait()


def solution(mesh):
    nr, nc = mesh.shape["row"], mesh.shape["col"]

    def local(queries, keys, values, grad_out, conv_weight):
        rows, width = queries.shape
        heads, nz = width // DH, nc // 2
        assert heads == nc
        scale = (DH * rows * nr * nc) ** (-0.5)
        vm, dma = pltpu.VMEM, pltpu.SemaphoreType.DMA
        hbm = pl.BlockSpec(memory_space=pl.ANY)
        wide = lambda n, t: vm((n, width), t)
        mats = lambda *n: vm((*n, DH, DH), BF16)
        out = jax.ShapeDtypeStruct((rows, width), BF16)
        return pl.pallas_call(
            functools.partial(kernel, nr, nc, scale),
            out_shape=(out, out, out, jax.ShapeDtypeStruct((CW, width), F32)),
            in_specs=[hbm, hbm, hbm, hbm, pl.BlockSpec(memory_space=pltpu.VMEM)],
            out_specs=[hbm] * 4,
            scratch_shapes=[
                wide(rows, BF16), wide(rows, BF16), wide(rows, BF16), wide(rows, BF16),
                wide(rows, BF16), wide(PAD + rows, F32), wide(TAIL, BF16),
                wide(rows + PAD, F32), wide(PAD, F32),
                wide(rows, F32), wide(rows, F32),
                wide(rows, BF16), wide(rows, BF16), wide(rows, BF16),
                mats(2, heads), mats(2, nz), mats(2, nz), mats(2, nz),
                mats(2), mats(nr), mats(2, nz), mats(2, nz), mats(2, nz), mats(2, heads),
                vm((heads, 8, DH), F32), vm((nc, 8, DH), F32), vm((8, DH), F32), vm((nr, 8, DH), F32),
                vm((8, DH), F32), vm((nc, 8, DH), F32), vm((CW, width), F32),
                dma((2, nz)), dma((2, nz)), dma((2, nz)), dma((2, nz)), dma((nr,)), dma((nr,)),
                dma((2, nz)), dma((2, nz)), dma((2, nz)), dma((2, nz)), dma((2,)), dma((2,)),
                dma((nc,)), dma((nc,)), dma((nr,)), dma((nr,)), dma((nc,)), dma((nc,)),
                dma((4,)), dma((4,)),
            ],
            compiler_params=pltpu.CompilerParams(collective_id=0, has_side_effects=True),
            name="linear_attention_backward",
        )(queries, keys, values, grad_out, conv_weight)

    tokens = P(("row", "col"), None)
    return jax.shard_map(
        local,
        mesh=mesh,
        in_specs=(tokens, tokens, tokens, tokens, P()),
        out_specs=(tokens, tokens, tokens, P()),
        check_vma=False,
    )
```

```python
import functools

import jax
import jax.numpy as jnp
from jax import lax
from jax.experimental import pallas as pl
from jax.experimental.pallas import tpu as pltpu
from jax.sharding import PartitionSpec as P

DH = 128
CW = 4
PAD = 8
TAIL = 16
MESH = pl.DeviceIdType.MESH
F32 = jnp.float32
BF16 = jnp.bfloat16
KEY, QUERY = 0, 1


def dot(a, b, contract):
    return lax.dot_general(a, b, ((contract[:1], contract[1:]), ((), ())), preferred_element_type=F32)


def kernel(
    nr, nc, scale,
    q_in, k_in, v_in, g_in, w_ref,
    gq_out, gk_out, gv_out, gw_out,
    q, k, v, g, conv, vext, vhalo, gext, ghalo, gq_part, gk_part, gq_v, gk_v, gv_v,
    state, sib_state, pair, zstate, total, rstate, back, zback, fwd, final,
    gw_part, gw_col, gw_row_src, gw_row, gw_all_src, gw_all, gw_v,
    sib_s, sib_r, zf_s, zf_r, row_s, row_r, zb_s, zb_r, sb_s, sb_r, halo_s, halo_r,
    cw_s, cw_r, rw_s, rw_r, aw_s, aw_r, in_sem, out_sem,
):
    r, c = lax.axis_index("row"), lax.axis_index("col")
    nz = nc // 2
    z, j = c // 2, c % 2
    rows, width = q.shape
    heads = width // DH
    sib = (r, 2 * z + (1 - j))
    place = r * nc + c
    blocks = nr * nc
    after, before = (place + 1) % blocks, (place + blocks - 1) % blocks
    after, before = (after // nc, after % nc), (before // nc, before % nc)
    far_first = sorted(range(1, nz), key=lambda o: -min(o, nz - o))
    near_first = far_first[::-1]

    def send(src, dst, ss, rs, to):
        return pltpu.make_async_remote_copy(src_ref=src, dst_ref=dst, send_sem=ss, recv_sem=rs, device_id=to, device_id_type=MESH)

    def at(o):
        return (z + o) % nz

    def lanes(h):
        return pl.ds(pl.multiple_of(h * DH, DH), DH)

    def each_head(fn, together=4, first=0, last=None):
        def some(i, carry):
            for u in range(together):
                fn(i * together + u)
            return carry

        lax.fori_loop(first // together, (heads if last is None else last) // together, some, 0)

    barrier = pltpu.get_barrier_semaphore()

    def greet(to):
        pl.semaphore_signal(barrier, inc=1, device_id=to, device_id_type=MESH)

    loads = [
        pltpu.make_async_copy(src, dst, in_sem.at[i])
        for i, (src, dst) in enumerate(((q_in, q), (g_in, g), (v_in, v), (k_in, k)))
    ]
    for load in loads:
        load.start()
    lax.fori_loop(1, nc, lambda o, x: (greet((r, (c + o) % nc)), x)[1], 0)
    lax.fori_loop(1, nr, lambda o, x: (greet(((r + o) % nr, c)), x)[1], 0)
    greet(after)
    greet(before)

    loads[0].wait()
    loads[1].wait()

    def query_state(h):
        state[QUERY, h] = dot(q[:, lanes(h)], g[:, lanes(h)], (0, 0)).astype(BF16)

    each_head(query_state)
    loads[3].wait()

    above = lax.broadcasted_iota(jnp.int32, (rows, rows), 0) <= lax.broadcasted_iota(jnp.int32, (rows, rows), 1)
    below = lax.broadcasted_iota(jnp.int32, (rows, rows), 0) >= lax.broadcasted_iota(jnp.int32, (rows, rows), 1)

    def score_part(h):
        score = jnp.where(above, dot(k[:, lanes(h)], q[:, lanes(h)], (1, 1)), 0.0).astype(BF16)
        gext[pl.ds(0, rows), lanes(h)] = dot(score, g[:, lanes(h)], (1, 0))

    each_head(score_part)

    loads[2].wait()
    vext[pl.ds(0, PAD)] = jnp.zeros((PAD, width), F32)

    def widen(h):
        vext[pl.ds(PAD, rows), lanes(h)] = v[:, lanes(h)].astype(F32)

    each_head(widen)
    pl.semaphore_wait(barrier, nc - 1 + nr - 1 + 2)

    vsend = send(v.at[pl.ds(rows - TAIL, TAIL)], vhalo, halo_s.at[0], halo_r.at[0], after)
    vsend.start()

    def to_sibling(kind, zz):
        send(
            state.at[kind, 2 * zz + (1 - j)], sib_state.at[kind, zz], sib_s.at[kind, zz], sib_r.at[kind, zz], sib
        ).start()

    for o in far_first + [0]:
        to_sibling(QUERY, at(o))

    def pair_up(kind):
        for o in far_first + [0]:
            zz = at(o)
            send(state.at[kind, 0], sib_state.at[kind, zz], sib_s.at[kind, zz], sib_r.at[kind, zz], sib).wait_recv()
            both = state[kind, 2 * zz + j].astype(F32) + sib_state[kind, zz].astype(F32)
            if o == 0:
                zstate[kind, zz] = both.astype(BF16)
            else:
                pair[kind, zz] = both.astype(BF16)
                send(
                    pair.at[kind, zz], zstate.at[kind, z], zf_s.at[kind, zz], zf_r.at[kind, z], (r, 2 * zz + j)
                ).start()

    def convolve(h, n=rows):
        total_ = jnp.zeros((n, DH), F32)
        for tap in range(CW):
            total_ = total_ + w_ref[pl.ds(tap, 1), lanes(h)] * vext[pl.ds(PAD - tap, n), lanes(h)]
        conv[pl.ds(0, n), lanes(h)] = total_.astype(BF16)

    each_head(convolve)
    pair_up(QUERY)

    send(v.at[pl.ds(rows - TAIL, TAIL)], vhalo, halo_s.at[0], halo_r.at[0], after).wait_recv()
    vext[pl.ds(0, PAD)] = jnp.where(place > 0, vhalo[pl.ds(TAIL - PAD, PAD)].astype(F32), 0.0)

    def key_state(h):
        convolve(h, TAIL)
        state[KEY, h] = dot(k[:, lanes(h)], conv[:, lanes(h)], (0, 0)).astype(BF16)

    for o in far_first + [0]:
        zz = at(o)
        key_state(2 * zz + (1 - j))
        to_sibling(KEY, zz)
    lax.fori_loop(0, nz, lambda i, x: (key_state(2 * i + j), x)[1], 0)
    pair_up(KEY)

    def attn_part(h):
        attn = jnp.where(below, dot(g[:, lanes(h)], conv[:, lanes(h)], (1, 1)), 0.0).astype(BF16)
        gq_part[:, lanes(h)] = dot(attn, k[:, lanes(h)], (1, 0))
        attn_t = jnp.where(above, dot(conv[:, lanes(h)], g[:, lanes(h)], (1, 1)), 0.0).astype(BF16)
        gk_part[:, lanes(h)] = dot(attn_t, q[:, lanes(h)], (1, 0))

    each_head(attn_part, last=4)

    def run_total(kind):
        acc = zstate[kind, z].astype(F32)
        for o in near_first:
            zz = at(o)
            send(pair.at[kind, 0], zstate.at[kind, zz], zf_s.at[kind, zz], zf_r.at[kind, zz], sib).wait_recv()
            acc = acc + zstate[kind, zz].astype(F32)
        total[kind] = acc.astype(BF16)

        def one(rr, x):
            send(total.at[kind], rstate.at[r], row_s.at[rr], row_r.at[r], (rr, c)).start()
            return x

        if kind == KEY:
            lax.fori_loop(r + 1, nr, one, 0)
        else:
            lax.fori_loop(0, r, one, 0)

    run_total(QUERY)
    each_head(attn_part, first=4)

    def spread(kind):
        def one(rr, acc):
            send(total.at[kind], rstate.at[rr], row_s.at[rr], row_r.at[rr], sib).wait_recv()
            return acc + rstate[rr].astype(F32)

        acc = jnp.zeros((DH, DH), F32)
        acc = lax.fori_loop(0, r, one, acc) if kind == KEY else lax.fori_loop(r + 1, nr, one, acc)
        for zz in range(nz) if kind == KEY else reversed(range(nz)):
            back[kind, zz] = acc.astype(BF16)
            acc = acc + zstate[kind, zz].astype(F32)
        for o in far_first:
            zz = at(o)
            send(
                back.at[kind, zz], zback.at[kind, z], zb_s.at[kind, zz], zb_r.at[kind, z], (r, 2 * zz + j)
            ).start()

    spread(QUERY)
    run_total(KEY)

    mine_too = {KEY: j.astype(F32), QUERY: (1 - j).astype(F32)}

    def arrive(kind, o):
        zz = at(o)
        h = 2 * zz + j
        if o == 0:
            chip = back[kind, zz].astype(F32)
        else:
            send(back.at[kind, 0], zback.at[kind, zz], zb_s.at[kind, zz], zb_r.at[kind, zz], sib).wait_recv()
            chip = zback[kind, zz].astype(F32)
        fwd[kind, zz] = (chip + (1.0 - mine_too[kind]) * state[kind, h].astype(F32)).astype(BF16)
        send(fwd.at[kind, zz], final.at[kind, h], sb_s.at[kind, zz], sb_r.at[kind, zz], sib).start()
        final[kind, h] = (chip + mine_too[kind] * sib_state[kind, zz].astype(F32)).astype(BF16)
        return h

    def arrive_other(kind, o):
        zz = at(o)
        h = 2 * zz + (1 - j)
        send(fwd.at[kind, 0], final.at[kind, h], sb_s.at[kind, zz], sb_r.at[kind, zz], sib).wait_recv()
        return h

    gw_part[...] = jnp.zeros_like(gw_part)

    def with_suffix(h):
        suffix = final[QUERY, h]
        grad_conv = scale * (gext[pl.ds(0, rows), lanes(h)] + dot(k[:, lanes(h)], suffix, (1, 0)))
        gext[pl.ds(0, rows), lanes(h)] = grad_conv
        for tap in range(CW):
            gw_part[h, pl.ds(tap, 1)] = jnp.sum(
                grad_conv * vext[pl.ds(PAD - tap, rows), lanes(h)], axis=0, keepdims=True
            )

    def weight_to_owner(h):
        send(gw_part.at[h], gw_col.at[c], cw_s.at[h], cw_r.at[c], (r, h)).start()

    for i, o in enumerate([0] + near_first):
        if i == 4:
            spread(KEY)
        h = arrive(QUERY, o)
        with_suffix(h)
        if o == 0:
            gw_col[c] = gw_part[h]
        else:
            weight_to_owner(h)
    for o in [0] + near_first:
        h = arrive_other(QUERY, o)
        with_suffix(h)
        weight_to_owner(h)
    gsend = send(gext.at[pl.ds(0, PAD)], ghalo, halo_s.at[1], halo_r.at[1], before)
    gsend.start()

    def grad_key(h):
        grad = scale * (gk_part[:, lanes(h)] + dot(conv[:, lanes(h)], final[QUERY, h], (1, 1)))
        gk_v[:, lanes(h)] = grad.astype(BF16)

    each_head(grad_key)
    gk_store = pltpu.make_async_copy(gk_v, gk_out, out_sem.at[0])
    gk_store.start()

    def from_col(o, acc):
        cc = (c + o) % nc
        send(gw_part.at[0], gw_col.at[cc], cw_s.at[cc], cw_r.at[cc], sib).wait_recv()
        return acc

    lax.fori_loop(1, nc, from_col, 0)
    gw_row_src[...] = jnp.sum(gw_col[...], axis=0)
    gw_row[r] = gw_row_src[...]

    def to_row(o, x):
        rr = (r + o) % nr
        send(gw_row_src, gw_row.at[r], rw_s.at[rr], rw_r.at[r], (rr, c)).start()
        return x

    lax.fori_loop(1, nr, to_row, 0)

    def with_prefix(h):
        grad_query = scale * (gq_part[:, lanes(h)] + dot(g[:, lanes(h)], final[KEY, h], (1, 1)))
        gq_v[:, lanes(h)] = grad_query.astype(BF16)

    for o in [0] + near_first:
        with_prefix(arrive(KEY, o))

    def from_row(o, x):
        rr = (r + o) % nr
        send(gw_row_src, gw_row.at[rr], rw_s.at[rr], rw_r.at[rr], sib).wait_recv()
        return x

    lax.fori_loop(1, nr, from_row, 0)
    gw_all_src[...] = jnp.sum(gw_row[...], axis=0)
    gw_all[c] = gw_all_src[...]

    def to_col(o, x):
        cc = (c + o) % nc
        send(gw_all_src, gw_all.at[c], aw_s.at[cc], aw_r.at[c], (r, cc)).start()
        return x

    lax.fori_loop(1, nc, to_col, 0)

    for o in [0] + near_first:
        with_prefix(arrive_other(KEY, o))
    gq_store = pltpu.make_async_copy(gq_v, gq_out, out_sem.at[1])
    gq_store.start()

    gsend.wait_recv()
    gext[pl.ds(rows, PAD)] = jnp.where(place < blocks - 1, ghalo[...], 0.0)

    def value_part(h):
        acc = jnp.zeros((rows, DH), F32)
        for tap in range(CW):
            acc = acc + w_ref[pl.ds(tap, 1), lanes(h)] * gext[pl.ds(tap, rows), lanes(h)]
        gv_v[:, lanes(h)] = acc.astype(BF16)

    each_head(value_part)
    gv_store = pltpu.make_async_copy(gv_v, gv_out, out_sem.at[2])
    gv_store.start()

    def from_all(o, x):
        cc = (c + o) % nc
        send(gw_all_src, gw_all.at[cc], aw_s.at[cc], aw_r.at[cc], sib).wait_recv()
        return x

    lax.fori_loop(1, nc, from_all, 0)
    for h in range(heads):
        gw_v[:, h * DH : (h + 1) * DH] = gw_all[h][:CW]
    gw_store = pltpu.make_async_copy(gw_v, gw_out, out_sem.at[3])
    gw_store.start()

    vsend.wait_send()
    gsend.wait_send()
    for kind in (KEY, QUERY):

        def sib_sent(i, x):
            send(state.at[kind, 0], sib_state.at[kind, 0], sib_s.at[kind, i], sib_r.at[kind, i], sib).wait_send()
            send(fwd.at[kind, 0], final.at[kind, 0], sb_s.at[kind, i], sb_r.at[kind, i], sib).wait_send()
            return x

        def z_sent(o, x):
            zz = (z + o) % nz
            send(pair.at[kind, 0], zstate.at[kind, 0], zf_s.at[kind, zz], zf_r.at[kind, zz], sib).wait_send()
            send(back.at[kind, 0], zback.at[kind, 0], zb_s.at[kind, zz], zb_r.at[kind, zz], sib).wait_send()
            return x

        lax.fori_loop(0, nz, sib_sent, 0)
        lax.fori_loop(1, nz, z_sent, 0)

    def row_sent(o, x):
        rr = (r + o) % nr
        send(total.at[0], rstate.at[0], row_s.at[rr], row_r.at[rr], sib).wait_send()
        send(gw_row_src, gw_row.at[0], rw_s.at[rr], rw_r.at[rr], sib).wait_send()
        return x

    def col_sent(o, x):
        cc = (c + o) % nc
        send(gw_part.at[0], gw_col.at[0], cw_s.at[cc], cw_r.at[cc], sib).wait_send()
        send(gw_all_src, gw_all.at[0], aw_s.at[cc], aw_r.at[cc], sib).wait_send()
        return x

    lax.fori_loop(1, nr, row_sent, 0)
    lax.fori_loop(1, nc, col_sent, 0)
    for store in (gk_store, gq_store, gv_store, gw_store):
        store.wait()


def solution(mesh):
    nr, nc = mesh.shape["row"], mesh.shape["col"]

    def local(queries, keys, values, grad_out, conv_weight):
        rows, width = queries.shape
        heads, nz = width // DH, nc // 2
        assert heads == nc
        scale = (DH * rows * nr * nc) ** (-0.5)
        vm, dma = pltpu.VMEM, pltpu.SemaphoreType.DMA
        hbm = pl.BlockSpec(memory_space=pl.ANY)
        wide = lambda n, t: vm((n, width), t)
        mats = lambda *n: vm((*n, DH, DH), BF16)
        out = jax.ShapeDtypeStruct((rows, width), BF16)
        return pl.pallas_call(
            functools.partial(kernel, nr, nc, scale),
            out_shape=(out, out, out, jax.ShapeDtypeStruct((CW, width), F32)),
            in_specs=[hbm, hbm, hbm, hbm, pl.BlockSpec(memory_space=pltpu.VMEM)],
            out_specs=[hbm] * 4,
            scratch_shapes=[
                wide(rows, BF16), wide(rows, BF16), wide(rows, BF16), wide(rows, BF16),
                wide(rows, BF16), wide(PAD + rows, F32), wide(TAIL, BF16),
                wide(rows + PAD, F32), wide(PAD, F32),
                wide(rows, F32), wide(rows, F32),
                wide(rows, BF16), wide(rows, BF16), wide(rows, BF16),
                mats(2, heads), mats(2, nz), mats(2, nz), mats(2, nz),
                mats(2), mats(nr), mats(2, nz), mats(2, nz), mats(2, nz), mats(2, heads),
                vm((heads, 8, DH), F32), vm((nc, 8, DH), F32), vm((8, DH), F32), vm((nr, 8, DH), F32),
                vm((8, DH), F32), vm((nc, 8, DH), F32), vm((CW, width), F32),
                dma((2, nz)), dma((2, nz)), dma((2, nz)), dma((2, nz)), dma((nr,)), dma((nr,)),
                dma((2, nz)), dma((2, nz)), dma((2, nz)), dma((2, nz)), dma((2,)), dma((2,)),
                dma((nc,)), dma((nc,)), dma((nr,)), dma((nr,)), dma((nc,)), dma((nc,)),
                dma((4,)), dma((4,)),
            ],
            compiler_params=pltpu.CompilerParams(collective_id=0, has_side_effects=True),
            name="linear_attention_backward",
        )(queries, keys, values, grad_out, conv_weight)

    tokens = P(("row", "col"), None)
    return jax.shard_map(
        local,
        mesh=mesh,
        in_specs=(tokens, tokens, tokens, tokens, P()),
        out_specs=(tokens, tokens, tokens, P()),
        check_vma=False,
    )
```

```python
import functools

import jax
import jax.numpy as jnp
from jax import lax
from jax.experimental import pallas as pl
from jax.experimental.pallas import tpu as pltpu
from jax.sharding import PartitionSpec as P

DH = 128
CW = 4
PAD = 8
TAIL = 16
MESH = pl.DeviceIdType.MESH
F32 = jnp.float32
BF16 = jnp.bfloat16
KEY, QUERY = 0, 1


def dot(a, b, contract):
    return lax.dot_general(a, b, ((contract[:1], contract[1:]), ((), ())), preferred_element_type=F32)


def kernel(
    nr, nc, scale,
    q_in, k_in, v_in, g_in, w_in,
    gq_out, gk_out, gv_out, gw_out,
    q, k, v, g, conv, vext, vhalo, gext, ghalo, gq_part, gk_part, gq_v, gk_v, gv_v,
    state, sib_state, pair, zstate, total, rstate, back, zback, fwd, final,
    gw_part, gw_col, gw_row_src, gw_row, gw_all_src, gw_all, gw_v, w_ref,
    sib_s, sib_r, zf_s, zf_r, row_s, row_r, zb_s, zb_r, sb_s, sb_r, halo_s, halo_r,
    cw_s, cw_r, rw_s, rw_r, aw_s, aw_r, in_sem, out_sem,
):
    r, c = lax.axis_index("row"), lax.axis_index("col")
    nz = nc // 2
    z, j = c // 2, c % 2
    rows, width = q.shape
    heads = width // DH
    sib = (r, 2 * z + (1 - j))
    place = r * nc + c
    blocks = nr * nc
    after, before = (place + 1) % blocks, (place + blocks - 1) % blocks
    after, before = (after // nc, after % nc), (before // nc, before % nc)
    far_first = sorted(range(1, nz), key=lambda o: -min(o, nz - o))
    near_first = far_first[::-1]

    def send(src, dst, ss, rs, to):
        return pltpu.make_async_remote_copy(src_ref=src, dst_ref=dst, send_sem=ss, recv_sem=rs, device_id=to, device_id_type=MESH)

    def at(o):
        return (z + o) % nz

    def lanes(h):
        return pl.ds(pl.multiple_of(h * DH, DH), DH)

    def each_head(fn, together=4):
        def some(i, carry):
            for u in range(together):
                fn(i * together + u)
            return carry

        lax.fori_loop(0, heads // together, some, 0)

    barrier = pltpu.get_barrier_semaphore()

    def greet(to):
        pl.semaphore_signal(barrier, inc=1, device_id=to, device_id_type=MESH)

    loads = [
        pltpu.make_async_copy(src, dst, in_sem.at[i])
        for i, (src, dst) in enumerate(((q_in, q), (g_in, g), (v_in, v), (k_in, k), (w_in, w_ref)))
    ]
    for load in loads:
        load.start()
    lax.fori_loop(1, nc, lambda o, x: (greet((r, (c + o) % nc)), x)[1], 0)
    lax.fori_loop(1, nr, lambda o, x: (greet(((r + o) % nr, c)), x)[1], 0)
    greet(after)
    greet(before)

    loads[0].wait()
    loads[1].wait()

    def query_state(h):
        state[QUERY, h] = dot(q[:, lanes(h)], g[:, lanes(h)], (0, 0)).astype(BF16)

    each_head(query_state)
    loads[2].wait()
    loads[3].wait()
    loads[4].wait()
    pl.semaphore_wait(barrier, nc - 1 + nr - 1 + 2)

    vsend = send(v.at[pl.ds(rows - TAIL, TAIL)], vhalo, halo_s.at[0], halo_r.at[0], after)
    vsend.start()

    def to_sibling(kind, zz):
        send(
            state.at[kind, 2 * zz + (1 - j)], sib_state.at[kind, zz], sib_s.at[kind, zz], sib_r.at[kind, zz], sib
        ).start()

    for o in far_first + [0]:
        to_sibling(QUERY, at(o))

    above = lax.broadcasted_iota(jnp.int32, (rows, rows), 0) <= lax.broadcasted_iota(jnp.int32, (rows, rows), 1)
    below = lax.broadcasted_iota(jnp.int32, (rows, rows), 0) >= lax.broadcasted_iota(jnp.int32, (rows, rows), 1)

    def score_part(h):
        score = jnp.where(above, dot(k[:, lanes(h)], q[:, lanes(h)], (1, 1)), 0.0).astype(BF16)
        gext[pl.ds(0, rows), lanes(h)] = dot(score, g[:, lanes(h)], (1, 0))

    each_head(score_part)

    def pair_up(kind):
        for o in far_first + [0]:
            zz = at(o)
            send(state.at[kind, 0], sib_state.at[kind, zz], sib_s.at[kind, zz], sib_r.at[kind, zz], sib).wait_recv()
            both = state[kind, 2 * zz + j].astype(F32) + sib_state[kind, zz].astype(F32)
            if o == 0:
                zstate[kind, zz] = both.astype(BF16)
            else:
                pair[kind, zz] = both.astype(BF16)
                send(
                    pair.at[kind, zz], zstate.at[kind, z], zf_s.at[kind, zz], zf_r.at[kind, z], (r, 2 * zz + j)
                ).start()

    pair_up(QUERY)

    send(v.at[pl.ds(rows - TAIL, TAIL)], vhalo, halo_s.at[0], halo_r.at[0], after).wait_recv()
    vext[pl.ds(0, PAD)] = jnp.where(place > 0, vhalo[pl.ds(TAIL - PAD, PAD)].astype(F32), 0.0)
    vext[pl.ds(PAD, rows)] = v[...].astype(F32)

    def convolve(h):
        total_ = jnp.zeros((rows, DH), F32)
        for tap in range(CW):
            total_ = total_ + w_ref[pl.ds(tap, 1), lanes(h)] * vext[pl.ds(PAD - tap, rows), lanes(h)]
        conv[:, lanes(h)] = total_.astype(BF16)

    def key_state(h):
        convolve(h)
        state[KEY, h] = dot(k[:, lanes(h)], conv[:, lanes(h)], (0, 0)).astype(BF16)

    for o in far_first + [0]:
        zz = at(o)
        key_state(2 * zz + (1 - j))
        to_sibling(KEY, zz)
    lax.fori_loop(0, nz, lambda i, x: (key_state(2 * i + j), x)[1], 0)
    pair_up(KEY)

    def attn_part(h):
        attn = jnp.where(below, dot(g[:, lanes(h)], conv[:, lanes(h)], (1, 1)), 0.0).astype(BF16)
        gq_part[:, lanes(h)] = dot(attn, k[:, lanes(h)], (1, 0))
        attn_t = jnp.where(above, dot(conv[:, lanes(h)], g[:, lanes(h)], (1, 1)), 0.0).astype(BF16)
        gk_part[:, lanes(h)] = dot(attn_t, q[:, lanes(h)], (1, 0))


    def run_total(kind):
        acc = zstate[kind, z].astype(F32)
        for o in near_first:
            zz = at(o)
            send(pair.at[kind, 0], zstate.at[kind, zz], zf_s.at[kind, zz], zf_r.at[kind, zz], sib).wait_recv()
            acc = acc + zstate[kind, zz].astype(F32)
        total[kind] = acc.astype(BF16)

        def one(rr, x):
            send(total.at[kind], rstate.at[r], row_s.at[rr], row_r.at[r], (rr, c)).start()
            return x

        if kind == KEY:
            lax.fori_loop(r + 1, nr, one, 0)
        else:
            lax.fori_loop(0, r, one, 0)

    run_total(QUERY)
    each_head(attn_part)
    run_total(KEY)

    def spread(kind):
        def one(rr, acc):
            send(total.at[kind], rstate.at[rr], row_s.at[rr], row_r.at[rr], sib).wait_recv()
            return acc + rstate[rr].astype(F32)

        acc = jnp.zeros((DH, DH), F32)
        acc = lax.fori_loop(0, r, one, acc) if kind == KEY else lax.fori_loop(r + 1, nr, one, acc)
        for zz in range(nz) if kind == KEY else reversed(range(nz)):
            back[kind, zz] = acc.astype(BF16)
            acc = acc + zstate[kind, zz].astype(F32)
        for o in far_first:
            zz = at(o)
            send(
                back.at[kind, zz], zback.at[kind, z], zb_s.at[kind, zz], zb_r.at[kind, z], (r, 2 * zz + j)
            ).start()

    spread(QUERY)
    spread(KEY)

    mine_too = {KEY: j.astype(F32), QUERY: (1 - j).astype(F32)}

    def arrive(kind, o):
        zz = at(o)
        h = 2 * zz + j
        if o == 0:
            chip = back[kind, zz].astype(F32)
        else:
            send(back.at[kind, 0], zback.at[kind, zz], zb_s.at[kind, zz], zb_r.at[kind, zz], sib).wait_recv()
            chip = zback[kind, zz].astype(F32)
        fwd[kind, zz] = (chip + (1.0 - mine_too[kind]) * state[kind, h].astype(F32)).astype(BF16)
        send(fwd.at[kind, zz], final.at[kind, h], sb_s.at[kind, zz], sb_r.at[kind, zz], sib).start()
        final[kind, h] = (chip + mine_too[kind] * sib_state[kind, zz].astype(F32)).astype(BF16)
        return h

    def arrive_other(kind, o):
        zz = at(o)
        h = 2 * zz + (1 - j)
        send(fwd.at[kind, 0], final.at[kind, h], sb_s.at[kind, zz], sb_r.at[kind, zz], sib).wait_recv()
        return h

    gw_part[...] = jnp.zeros_like(gw_part)

    def with_suffix(h):
        suffix = final[QUERY, h]
        grad_conv = scale * (gext[pl.ds(0, rows), lanes(h)] + dot(k[:, lanes(h)], suffix, (1, 0)))
        gext[pl.ds(0, rows), lanes(h)] = grad_conv
        grad_key = scale * (gk_part[:, lanes(h)] + dot(conv[:, lanes(h)], suffix, (1, 1)))
        gk_v[:, lanes(h)] = grad_key.astype(BF16)
        for tap in range(CW):
            gw_part[h, pl.ds(tap, 1)] = jnp.sum(
                grad_conv * vext[pl.ds(PAD - tap, rows), lanes(h)], axis=0, keepdims=True
            )

    def weight_to_owner(h):
        send(gw_part.at[h], gw_col.at[c], cw_s.at[h], cw_r.at[c], (r, h)).start()

    for o in [0] + near_first:
        h = arrive(QUERY, o)
        with_suffix(h)
        if o == 0:
            gw_col[c] = gw_part[h]
        else:
            weight_to_owner(h)
    for o in [0] + near_first:
        h = arrive_other(QUERY, o)
        with_suffix(h)
        weight_to_owner(h)
    gsend = send(gext.at[pl.ds(0, PAD)], ghalo, halo_s.at[1], halo_r.at[1], before)
    gsend.start()
    gk_store = pltpu.make_async_copy(gk_v, gk_out, out_sem.at[0])
    gk_store.start()

    def from_col(o, acc):
        cc = (c + o) % nc
        send(gw_part.at[0], gw_col.at[cc], cw_s.at[cc], cw_r.at[cc], sib).wait_recv()
        return acc

    lax.fori_loop(1, nc, from_col, 0)
    gw_row_src[...] = jnp.sum(gw_col[...], axis=0)
    gw_row[r] = gw_row_src[...]

    def to_row(o, x):
        rr = (r + o) % nr
        send(gw_row_src, gw_row.at[r], rw_s.at[rr], rw_r.at[r], (rr, c)).start()
        return x

    lax.fori_loop(1, nr, to_row, 0)

    def with_prefix(h):
        grad_query = scale * (gq_part[:, lanes(h)] + dot(g[:, lanes(h)], final[KEY, h], (1, 1)))
        gq_v[:, lanes(h)] = grad_query.astype(BF16)

    for o in [0] + near_first:
        with_prefix(arrive(KEY, o))

    def from_row(o, x):
        rr = (r + o) % nr
        send(gw_row_src, gw_row.at[rr], rw_s.at[rr], rw_r.at[rr], sib).wait_recv()
        return x

    lax.fori_loop(1, nr, from_row, 0)
    gw_all_src[...] = jnp.sum(gw_row[...], axis=0)
    gw_all[c] = gw_all_src[...]

    def to_col(o, x):
        cc = (c + o) % nc
        send(gw_all_src, gw_all.at[c], aw_s.at[cc], aw_r.at[c], (r, cc)).start()
        return x

    lax.fori_loop(1, nc, to_col, 0)

    for o in [0] + near_first:
        with_prefix(arrive_other(KEY, o))
    gq_store = pltpu.make_async_copy(gq_v, gq_out, out_sem.at[1])
    gq_store.start()

    gsend.wait_recv()
    gext[pl.ds(rows, PAD)] = jnp.where(place < blocks - 1, ghalo[...], 0.0)

    def value_part(h):
        acc = jnp.zeros((rows, DH), F32)
        for tap in range(CW):
            acc = acc + w_ref[pl.ds(tap, 1), lanes(h)] * gext[pl.ds(tap, rows), lanes(h)]
        gv_v[:, lanes(h)] = acc.astype(BF16)

    each_head(value_part)
    gv_store = pltpu.make_async_copy(gv_v, gv_out, out_sem.at[2])
    gv_store.start()

    def from_all(o, x):
        cc = (c + o) % nc
        send(gw_all_src, gw_all.at[cc], aw_s.at[cc], aw_r.at[cc], sib).wait_recv()
        return x

    lax.fori_loop(1, nc, from_all, 0)
    for h in range(heads):
        gw_v[:, h * DH : (h + 1) * DH] = gw_all[h][:CW]
    gw_store = pltpu.make_async_copy(gw_v, gw_out, out_sem.at[3])
    gw_store.start()

    vsend.wait_send()
    gsend.wait_send()
    for kind in (KEY, QUERY):

        def sib_sent(i, x):
            send(state.at[kind, 0], sib_state.at[kind, 0], sib_s.at[kind, i], sib_r.at[kind, i], sib).wait_send()
            send(fwd.at[kind, 0], final.at[kind, 0], sb_s.at[kind, i], sb_r.at[kind, i], sib).wait_send()
            return x

        def z_sent(o, x):
            zz = (z + o) % nz
            send(pair.at[kind, 0], zstate.at[kind, 0], zf_s.at[kind, zz], zf_r.at[kind, zz], sib).wait_send()
            send(back.at[kind, 0], zback.at[kind, 0], zb_s.at[kind, zz], zb_r.at[kind, zz], sib).wait_send()
            return x

        lax.fori_loop(0, nz, sib_sent, 0)
        lax.fori_loop(1, nz, z_sent, 0)

    def row_sent(o, x):
        rr = (r + o) % nr
        send(total.at[0], rstate.at[0], row_s.at[rr], row_r.at[rr], sib).wait_send()
        send(gw_row_src, gw_row.at[0], rw_s.at[rr], rw_r.at[rr], sib).wait_send()
        return x

    def col_sent(o, x):
        cc = (c + o) % nc
        send(gw_part.at[0], gw_col.at[0], cw_s.at[cc], cw_r.at[cc], sib).wait_send()
        send(gw_all_src, gw_all.at[0], aw_s.at[cc], aw_r.at[cc], sib).wait_send()
        return x

    lax.fori_loop(1, nr, row_sent, 0)
    lax.fori_loop(1, nc, col_sent, 0)
    for store in (gk_store, gq_store, gv_store, gw_store):
        store.wait()


def put_out(*refs):
    n = (len(refs) - 2) // 3
    src, dst, held, (in_sem, out_sem) = refs[:n], refs[n : 2 * n], refs[2 * n : 3 * n], refs[3 * n :]
    loads = [pltpu.make_async_copy(src[i], held[i], in_sem.at[i]) for i in range(n)]
    stores = [pltpu.make_async_copy(held[i], dst[i], out_sem.at[i]) for i in range(n)]
    for load in loads:
        load.start()
    for load, store in zip(loads, stores):
        load.wait()
        store.start()
    for store in stores:
        store.wait()


def solution(mesh):
    nr, nc = mesh.shape["row"], mesh.shape["col"]

    def local(queries, keys, values, grad_out, conv_weight):
        rows, width = queries.shape
        heads, nz = width // DH, nc // 2
        assert heads == nc
        scale = (DH * rows * nr * nc) ** (-0.5)
        vm, dma = pltpu.VMEM, pltpu.SemaphoreType.DMA
        hbm = pl.BlockSpec(memory_space=pl.ANY)
        wide = lambda n, t: vm((n, width), t)
        mats = lambda *n: vm((*n, DH, DH), BF16)
        out = jax.ShapeDtypeStruct((rows, width), BF16)
        outs = (out, out, out, jax.ShapeDtypeStruct((CW, width), F32))
        results = pl.pallas_call(
            functools.partial(kernel, nr, nc, scale),
            out_shape=outs,
            in_specs=[hbm] * 5,
            out_specs=[hbm] * 4,
            scratch_shapes=[
                wide(rows, BF16), wide(rows, BF16), wide(rows, BF16), wide(rows, BF16),
                wide(rows, BF16), wide(PAD + rows, F32), wide(TAIL, BF16),
                wide(rows + PAD, F32), wide(PAD, F32),
                wide(rows, F32), wide(rows, F32),
                wide(rows, BF16), wide(rows, BF16), wide(rows, BF16),
                mats(2, heads), mats(2, nz), mats(2, nz), mats(2, nz),
                mats(2), mats(nr), mats(2, nz), mats(2, nz), mats(2, nz), mats(2, heads),
                vm((heads, 8, DH), F32), vm((nc, 8, DH), F32), vm((8, DH), F32), vm((nr, 8, DH), F32),
                vm((8, DH), F32), vm((nc, 8, DH), F32), vm((CW, width), F32), vm((CW, width), F32),
                dma((2, nz)), dma((2, nz)), dma((2, nz)), dma((2, nz)), dma((nr,)), dma((nr,)),
                dma((2, nz)), dma((2, nz)), dma((2, nz)), dma((2, nz)), dma((2,)), dma((2,)),
                dma((nc,)), dma((nc,)), dma((nr,)), dma((nr,)), dma((nc,)), dma((nc,)),
                dma((5,)), dma((4,)),
            ],
            compiler_params=pltpu.CompilerParams(collective_id=0, has_side_effects=True),
            name="linear_attention_backward",
        )(queries, keys, values, grad_out, conv_weight)
        return pl.pallas_call(
            put_out,
            out_shape=outs,
            in_specs=[hbm] * 4,
            out_specs=[hbm] * 4,
            scratch_shapes=[vm(o.shape, o.dtype) for o in outs] + [dma((4,)), dma((4,))],
            name="put_out",
        )(*results)

    tokens = P(("row", "col"), None)
    return jax.shard_map(
        local,
        mesh=mesh,
        in_specs=(tokens, tokens, tokens, tokens, P()),
        out_specs=(tokens, tokens, tokens, P()),
        check_vma=False,
    )
```

```python
import functools

import jax
import jax.numpy as jnp
from jax import lax
from jax.experimental import pallas as pl
from jax.experimental.pallas import tpu as pltpu
from jax.sharding import PartitionSpec as P

DH = 128
CW = 4
PAD = 8
TAIL = 16
PIECES = 4
MESH = pl.DeviceIdType.MESH
F32 = jnp.float32
BF16 = jnp.bfloat16
KEY, QUERY = 0, 1


def dot(a, b, contract):
    return lax.dot_general(a, b, ((contract[:1], contract[1:]), ((), ())), preferred_element_type=F32)


def kernel(
    nr, nc, scale,
    q_in, k_in, v_in, g_in, w_in,
    gq_out, gk_out, gv_out, gw_out,
    q, k, v, g, conv, vext, vhalo, gext, ghalo, gq_part, gk_part, gq_v, gk_v, gv_v,
    state, sib_state, pair, zstate, total, rstate, back, zback, fwd, final,
    gw_part, gw_col, gw_row_src, gw_row, gw_all_src, gw_all, gw_v, w_ref,
    sib_s, sib_r, zf_s, zf_r, row_s, row_r, zb_s, zb_r, sb_s, sb_r, halo_s, halo_r,
    cw_s, cw_r, rw_s, rw_r, aw_s, aw_r, in_sem, out_sem,
):
    r, c = lax.axis_index("row"), lax.axis_index("col")
    nz = nc // 2
    z, j = c // 2, c % 2
    rows, width = q.shape
    heads = width // DH
    sib = (r, 2 * z + (1 - j))
    place = r * nc + c
    blocks = nr * nc
    after, before = (place + 1) % blocks, (place + blocks - 1) % blocks
    after, before = (after // nc, after % nc), (before // nc, before % nc)
    far_first = sorted(range(1, nz), key=lambda o: -min(o, nz - o))
    near_first = far_first[::-1]

    def send(src, dst, ss, rs, to):
        return pltpu.make_async_remote_copy(src_ref=src, dst_ref=dst, send_sem=ss, recv_sem=rs, device_id=to, device_id_type=MESH)

    def at(o):
        return (z + o) % nz

    def lanes(h):
        return pl.ds(pl.multiple_of(h * DH, DH), DH)

    def each_head(fn, together=4):
        def some(i, carry):
            for u in range(together):
                fn(i * together + u)
            return carry

        lax.fori_loop(0, heads // together, some, 0)

    barrier = pltpu.get_barrier_semaphore()

    def greet(to):
        pl.semaphore_signal(barrier, inc=1, device_id=to, device_id_type=MESH)

    loads = [
        pltpu.make_async_copy(src, dst, in_sem.at[i])
        for i, (src, dst) in enumerate(((q_in, q), (g_in, g), (v_in, v), (k_in, k), (w_in, w_ref)))
    ]
    for load in loads:
        load.start()
    lax.fori_loop(1, nc, lambda o, x: (greet((r, (c + o) % nc)), x)[1], 0)
    lax.fori_loop(1, nr, lambda o, x: (greet(((r + o) % nr, c)), x)[1], 0)
    greet(after)
    greet(before)

    loads[0].wait()
    loads[1].wait()

    def query_state(h):
        state[QUERY, h] = dot(q[:, lanes(h)], g[:, lanes(h)], (0, 0)).astype(BF16)

    each_head(query_state)
    loads[2].wait()
    loads[3].wait()
    loads[4].wait()
    pl.semaphore_wait(barrier, nc - 1 + nr - 1 + 2)

    vsend = send(v.at[pl.ds(rows - TAIL, TAIL)], vhalo, halo_s.at[0], halo_r.at[0], after)
    vsend.start()

    def to_sibling(kind, zz):
        send(
            state.at[kind, 2 * zz + (1 - j)], sib_state.at[kind, zz], sib_s.at[kind, zz], sib_r.at[kind, zz], sib
        ).start()

    for o in far_first + [0]:
        to_sibling(QUERY, at(o))

    above = lax.broadcasted_iota(jnp.int32, (rows, rows), 0) <= lax.broadcasted_iota(jnp.int32, (rows, rows), 1)
    below = lax.broadcasted_iota(jnp.int32, (rows, rows), 0) >= lax.broadcasted_iota(jnp.int32, (rows, rows), 1)

    def score_part(h):
        score = jnp.where(above, dot(k[:, lanes(h)], q[:, lanes(h)], (1, 1)), 0.0).astype(BF16)
        gext[pl.ds(0, rows), lanes(h)] = dot(score, g[:, lanes(h)], (1, 0))


    def pair_up(kind):
        for o in far_first + [0]:
            zz = at(o)
            send(state.at[kind, 0], sib_state.at[kind, zz], sib_s.at[kind, zz], sib_r.at[kind, zz], sib).wait_recv()
            both = state[kind, 2 * zz + j].astype(F32) + sib_state[kind, zz].astype(F32)
            if o == 0:
                zstate[kind, zz] = both.astype(BF16)
            else:
                pair[kind, zz] = both.astype(BF16)
                send(
                    pair.at[kind, zz], zstate.at[kind, z], zf_s.at[kind, zz], zf_r.at[kind, z], (r, 2 * zz + j)
                ).start()

    pair_up(QUERY)

    send(v.at[pl.ds(rows - TAIL, TAIL)], vhalo, halo_s.at[0], halo_r.at[0], after).wait_recv()
    vext[pl.ds(0, PAD)] = jnp.where(place > 0, vhalo[pl.ds(TAIL - PAD, PAD)].astype(F32), 0.0)
    vext[pl.ds(PAD, rows)] = v[...].astype(F32)

    def convolve(h):
        total_ = jnp.zeros((rows, DH), F32)
        for tap in range(CW):
            total_ = total_ + w_ref[pl.ds(tap, 1), lanes(h)] * vext[pl.ds(PAD - tap, rows), lanes(h)]
        conv[:, lanes(h)] = total_.astype(BF16)

    def key_state(h):
        convolve(h)
        state[KEY, h] = dot(k[:, lanes(h)], conv[:, lanes(h)], (0, 0)).astype(BF16)

    for o in far_first + [0]:
        zz = at(o)
        key_state(2 * zz + (1 - j))
        to_sibling(KEY, zz)
    lax.fori_loop(0, nz, lambda i, x: (key_state(2 * i + j), x)[1], 0)
    pair_up(KEY)
    each_head(score_part)

    def attn_part(h):
        attn = jnp.where(below, dot(g[:, lanes(h)], conv[:, lanes(h)], (1, 1)), 0.0).astype(BF16)
        gq_part[:, lanes(h)] = dot(attn, k[:, lanes(h)], (1, 0))
        attn_t = jnp.where(above, dot(conv[:, lanes(h)], g[:, lanes(h)], (1, 1)), 0.0).astype(BF16)
        gk_part[:, lanes(h)] = dot(attn_t, q[:, lanes(h)], (1, 0))


    def run_total(kind):
        acc = zstate[kind, z].astype(F32)
        for o in near_first:
            zz = at(o)
            send(pair.at[kind, 0], zstate.at[kind, zz], zf_s.at[kind, zz], zf_r.at[kind, zz], sib).wait_recv()
            acc = acc + zstate[kind, zz].astype(F32)
        total[kind] = acc.astype(BF16)

        def one(rr, x):
            send(total.at[kind], rstate.at[r], row_s.at[rr], row_r.at[r], (rr, c)).start()
            return x

        if kind == KEY:
            lax.fori_loop(r + 1, nr, one, 0)
        else:
            lax.fori_loop(0, r, one, 0)

    run_total(QUERY)
    each_head(attn_part)
    run_total(KEY)

    def spread(kind):
        def one(rr, acc):
            send(total.at[kind], rstate.at[rr], row_s.at[rr], row_r.at[rr], sib).wait_recv()
            return acc + rstate[rr].astype(F32)

        acc = jnp.zeros((DH, DH), F32)
        acc = lax.fori_loop(0, r, one, acc) if kind == KEY else lax.fori_loop(r + 1, nr, one, acc)
        for zz in range(nz) if kind == KEY else reversed(range(nz)):
            back[kind, zz] = acc.astype(BF16)
            acc = acc + zstate[kind, zz].astype(F32)
        for o in far_first:
            zz = at(o)
            send(
                back.at[kind, zz], zback.at[kind, z], zb_s.at[kind, zz], zb_r.at[kind, z], (r, 2 * zz + j)
            ).start()

    spread(QUERY)
    spread(KEY)

    mine_too = {KEY: j.astype(F32), QUERY: (1 - j).astype(F32)}

    def arrive(kind, o):
        zz = at(o)
        h = 2 * zz + j
        if o == 0:
            chip = back[kind, zz].astype(F32)
        else:
            send(back.at[kind, 0], zback.at[kind, zz], zb_s.at[kind, zz], zb_r.at[kind, zz], sib).wait_recv()
            chip = zback[kind, zz].astype(F32)
        fwd[kind, zz] = (chip + (1.0 - mine_too[kind]) * state[kind, h].astype(F32)).astype(BF16)
        send(fwd.at[kind, zz], final.at[kind, h], sb_s.at[kind, zz], sb_r.at[kind, zz], sib).start()
        final[kind, h] = (chip + mine_too[kind] * sib_state[kind, zz].astype(F32)).astype(BF16)
        return h

    def arrive_other(kind, o):
        zz = at(o)
        h = 2 * zz + (1 - j)
        send(fwd.at[kind, 0], final.at[kind, h], sb_s.at[kind, zz], sb_r.at[kind, zz], sib).wait_recv()
        return h

    gw_part[...] = jnp.zeros_like(gw_part)

    def with_suffix(h):
        suffix = final[QUERY, h]
        grad_conv = scale * (gext[pl.ds(0, rows), lanes(h)] + dot(k[:, lanes(h)], suffix, (1, 0)))
        gext[pl.ds(0, rows), lanes(h)] = grad_conv
        for tap in range(CW):
            gw_part[h, pl.ds(tap, 1)] = jnp.sum(
                grad_conv * vext[pl.ds(PAD - tap, rows), lanes(h)], axis=0, keepdims=True
            )

    def weight_to_owner(h):
        send(gw_part.at[h], gw_col.at[c], cw_s.at[h], cw_r.at[c], (r, h)).start()

    for o in [0] + near_first:
        h = arrive(QUERY, o)
        with_suffix(h)
        if o == 0:
            gw_col[c] = gw_part[h]
        else:
            weight_to_owner(h)
    for o in [0] + near_first:
        h = arrive_other(QUERY, o)
        with_suffix(h)
        weight_to_owner(h)
    gsend = send(gext.at[pl.ds(0, PAD)], ghalo, halo_s.at[1], halo_r.at[1], before)
    gsend.start()

    def grad_key(h):
        grad = scale * (gk_part[:, lanes(h)] + dot(conv[:, lanes(h)], final[QUERY, h], (1, 1)))
        gk_v[:, lanes(h)] = grad.astype(BF16)

    each_head(grad_key)
    gk_store = pltpu.make_async_copy(gk_v, gk_out, out_sem.at[0])
    gk_store.start()

    def from_col(o, acc):
        cc = (c + o) % nc
        send(gw_part.at[0], gw_col.at[cc], cw_s.at[cc], cw_r.at[cc], sib).wait_recv()
        return acc

    lax.fori_loop(1, nc, from_col, 0)
    gw_row_src[...] = jnp.sum(gw_col[...], axis=0)
    gw_row[r] = gw_row_src[...]

    def to_row(o, x):
        rr = (r + o) % nr
        send(gw_row_src, gw_row.at[r], rw_s.at[rr], rw_r.at[r], (rr, c)).start()
        return x

    lax.fori_loop(1, nr, to_row, 0)

    def with_prefix(h):
        grad_query = scale * (gq_part[:, lanes(h)] + dot(g[:, lanes(h)], final[KEY, h], (1, 1)))
        gq_v[:, lanes(h)] = grad_query.astype(BF16)

    for o in [0] + near_first:
        with_prefix(arrive(KEY, o))

    def from_row(o, x):
        rr = (r + o) % nr
        send(gw_row_src, gw_row.at[rr], rw_s.at[rr], rw_r.at[rr], sib).wait_recv()
        return x

    lax.fori_loop(1, nr, from_row, 0)
    gw_all_src[...] = jnp.sum(gw_row[...], axis=0)
    gw_all[c] = gw_all_src[...]

    def to_col(o, x):
        cc = (c + o) % nc
        send(gw_all_src, gw_all.at[c], aw_s.at[cc], aw_r.at[c], (r, cc)).start()
        return x

    lax.fori_loop(1, nc, to_col, 0)

    for o in [0] + near_first:
        with_prefix(arrive_other(KEY, o))
    gq_store = pltpu.make_async_copy(gq_v, gq_out, out_sem.at[1])
    gq_store.start()

    gsend.wait_recv()
    gext[pl.ds(rows, PAD)] = jnp.where(place < blocks - 1, ghalo[...], 0.0)

    def value_part(h):
        acc = jnp.zeros((rows, DH), F32)
        for tap in range(CW):
            acc = acc + w_ref[pl.ds(tap, 1), lanes(h)] * gext[pl.ds(tap, rows), lanes(h)]
        gv_v[:, lanes(h)] = acc.astype(BF16)

    each_head(value_part)
    gv_store = pltpu.make_async_copy(gv_v, gv_out, out_sem.at[2])
    gv_store.start()

    def from_all(o, x):
        cc = (c + o) % nc
        send(gw_all_src, gw_all.at[cc], aw_s.at[cc], aw_r.at[cc], sib).wait_recv()
        return x

    lax.fori_loop(1, nc, from_all, 0)
    for h in range(heads):
        gw_v[:, h * DH : (h + 1) * DH] = gw_all[h][:CW]
    gw_store = pltpu.make_async_copy(gw_v, gw_out, out_sem.at[3])
    gw_store.start()

    vsend.wait_send()
    gsend.wait_send()
    for kind in (KEY, QUERY):

        def sib_sent(i, x):
            send(state.at[kind, 0], sib_state.at[kind, 0], sib_s.at[kind, i], sib_r.at[kind, i], sib).wait_send()
            send(fwd.at[kind, 0], final.at[kind, 0], sb_s.at[kind, i], sb_r.at[kind, i], sib).wait_send()
            return x

        def z_sent(o, x):
            zz = (z + o) % nz
            send(pair.at[kind, 0], zstate.at[kind, 0], zf_s.at[kind, zz], zf_r.at[kind, zz], sib).wait_send()
            send(back.at[kind, 0], zback.at[kind, 0], zb_s.at[kind, zz], zb_r.at[kind, zz], sib).wait_send()
            return x

        lax.fori_loop(0, nz, sib_sent, 0)
        lax.fori_loop(1, nz, z_sent, 0)

    def row_sent(o, x):
        rr = (r + o) % nr
        send(total.at[0], rstate.at[0], row_s.at[rr], row_r.at[rr], sib).wait_send()
        send(gw_row_src, gw_row.at[0], rw_s.at[rr], rw_r.at[rr], sib).wait_send()
        return x

    def col_sent(o, x):
        cc = (c + o) % nc
        send(gw_part.at[0], gw_col.at[0], cw_s.at[cc], cw_r.at[cc], sib).wait_send()
        send(gw_all_src, gw_all.at[0], aw_s.at[cc], aw_r.at[cc], sib).wait_send()
        return x

    lax.fori_loop(1, nr, row_sent, 0)
    lax.fori_loop(1, nc, col_sent, 0)
    for store in (gk_store, gq_store, gv_store, gw_store):
        store.wait()


def put_out(*refs):
    n = (len(refs) - 2) // 3
    src, dst, held, (in_sem, out_sem) = refs[:n], refs[n : 2 * n], refs[2 * n : 3 * n], refs[3 * n :]
    loads, stores = [], []
    for i in range(n):
        rows = src[i].shape[0]
        step = rows // PIECES if rows % (TAIL * PIECES) == 0 else rows
        for p in range(rows // step):
            part = pl.ds(p * step, step)
            loads.append(pltpu.make_async_copy(src[i].at[part], held[i].at[part], in_sem.at[i, p]))
            stores.append(pltpu.make_async_copy(held[i].at[part], dst[i].at[part], out_sem.at[i, p]))
    for load in loads:
        load.start()
    for load, store in zip(loads, stores):
        load.wait()
        store.start()
    for store in stores:
        store.wait()


def solution(mesh):
    nr, nc = mesh.shape["row"], mesh.shape["col"]

    def local(queries, keys, values, grad_out, conv_weight):
        rows, width = queries.shape
        heads, nz = width // DH, nc // 2
        assert heads == nc
        scale = (DH * rows * nr * nc) ** (-0.5)
        vm, dma = pltpu.VMEM, pltpu.SemaphoreType.DMA
        hbm = pl.BlockSpec(memory_space=pl.ANY)
        wide = lambda n, t: vm((n, width), t)
        mats = lambda *n: vm((*n, DH, DH), BF16)
        out = jax.ShapeDtypeStruct((rows, width), BF16)
        outs = (out, out, out, jax.ShapeDtypeStruct((CW, width), F32))
        results = pl.pallas_call(
            functools.partial(kernel, nr, nc, scale),
            out_shape=outs,
            in_specs=[hbm] * 5,
            out_specs=[hbm] * 4,
            scratch_shapes=[
                wide(rows, BF16), wide(rows, BF16), wide(rows, BF16), wide(rows, BF16),
                wide(rows, BF16), wide(PAD + rows, F32), wide(TAIL, BF16),
                wide(rows + PAD, F32), wide(PAD, F32),
                wide(rows, F32), wide(rows, F32),
                wide(rows, BF16), wide(rows, BF16), wide(rows, BF16),
                mats(2, heads), mats(2, nz), mats(2, nz), mats(2, nz),
                mats(2), mats(nr), mats(2, nz), mats(2, nz), mats(2, nz), mats(2, heads),
                vm((heads, 8, DH), F32), vm((nc, 8, DH), F32), vm((8, DH), F32), vm((nr, 8, DH), F32),
                vm((8, DH), F32), vm((nc, 8, DH), F32), vm((CW, width), F32), vm((CW, width), F32),
                dma((2, nz)), dma((2, nz)), dma((2, nz)), dma((2, nz)), dma((nr,)), dma((nr,)),
                dma((2, nz)), dma((2, nz)), dma((2, nz)), dma((2, nz)), dma((2,)), dma((2,)),
                dma((nc,)), dma((nc,)), dma((nr,)), dma((nr,)), dma((nc,)), dma((nc,)),
                dma((5,)), dma((4,)),
            ],
            compiler_params=pltpu.CompilerParams(collective_id=0, has_side_effects=True),
            name="linear_attention_backward",
        )(queries, keys, values, grad_out, conv_weight)
        return pl.pallas_call(
            put_out,
            out_shape=outs,
            in_specs=[hbm] * 4,
            out_specs=[hbm] * 4,
            scratch_shapes=[vm(o.shape, o.dtype) for o in outs] + [dma((4, PIECES))] * 2,
            name="put_out",
        )(*results)

    tokens = P(("row", "col"), None)
    return jax.shard_map(
        local,
        mesh=mesh,
        in_specs=(tokens, tokens, tokens, tokens, P()),
        out_specs=(tokens, tokens, tokens, P()),
        check_vma=False,
    )
```
